32 devices in a mesh: gx: 4 (over z), gy: 2 (over core), gz: 4 (over y, x).
Axes of the slice: x: 2, y: 2, z: 4, core: 2. Of those that a mesh axis runs over, the one named last changes fastest.
Arguments:
- species: float32 [32, 16, 32, 256], P('gx', 'gy', 'gz'), may hold values from 0.25 to 4
- substeps: int32 [16, 2, 4], P('gx', 'gy', 'gz'), may hold values from 1 to 4, as said below
- reactants: int32 [1024, 256], replicated, may hold values from 0 to 2, as said below
- products: int32 [1024, 256], replicated, may hold values from 0 to 2, as said below
- rate_const: float32 [1024], replicated, may hold values from 0.01 to 0.2
- velocity: float32 [3, 32, 16, 32], P(None, 'gx', 'gy', 'gz'), may hold values from -0.3 to 0.3
- viscosity: float32 [32, 16, 32], P('gx', 'gy', 'gz'), may hold values from 0.25 to 1
- diffusivity: float32 [256], replicated, may hold values from 0.03 to 0.12
Outputs:
- evolved: float32 [32, 16, 32, 256], P('gx', 'gy', 'gz')
The draws below stay inside these ranges and needn't reach their ends.
Inputs may be any that keep to these rules, and one draw needn't show every extreme that they name: `substeps`: one entry for each block of 128 cells (2 x-planes of a brick); the value 4 occurs in every draw. `reactants`: each row sums to 2. `products`: each row sums to 2.
All inputs are finite; a program needn't handle non-finite values.
Results may differ from the reference program's by a relative error of at most 0.00077.
Values sent between devices are 32-bit elements; how exact they have to be, the bound alone decides.
No kernel may reach another device: no remote copies, remote signals or barrier semaphores. Data moves between devices by JAX's collectives and lax.ppermute only.
A program may use at most 64 MiB of HBM per device.

```python
import math
import jax
import jax.numpy as jnp
from jax import lax

S = 256
R = 1024
BY = 8
BZ = 8
BLOCK = 128
MAX_SUB = 4
PLANES = 2
NX = 32
NY = 16
NZ = 32
BLK_X = 16
BLK_Y = 2
BLK_Z = 4


def draw_substeps(key, part):
    key_center = jax.random.fold_in(key, 101)
    key_flame = jax.random.fold_in(key, 202)
    key_quiet = jax.random.fold_in(key, 303)
    center = jax.random.randint(key_center, (), 0, BLK_X)
    blocks = jnp.arange(BLK_X)
    flame_mask = (blocks - center) % BLK_X < max(BLK_X // 8, 1)
    flame_counts = jax.random.randint(key_flame, (BLK_X, BLK_Y, BLK_Z), 3, 5)
    quiet_counts = jax.random.randint(key_quiet, (BLK_X, BLK_Y, BLK_Z), 1, 3)
    counts = jnp.where(flame_mask[:, None, None], flame_counts, quiet_counts)
    counts = counts.at[center, 0, 0].set(4)
    return counts.astype(jnp.int32)


def pick_matrix(key):
    slots = jax.random.randint(key, (R, 2), 0, S)
    slots = slots.at[0, 1].set(slots[0, 0])
    species_ids = jnp.arange(S)
    matrix = (slots[:, 0:1] == species_ids[None, :]).astype(jnp.int32) + (slots[:, 1:2] == species_ids[None, :]).astype(jnp.int32)
    return matrix.astype(jnp.int32)


def draw_reactants(key, part):
    return pick_matrix(jax.random.fold_in(key, 11))


def draw_products(key, part):
    return pick_matrix(jax.random.fold_in(key, 23))


def steps_of(rng, dims, pieces, smallest, top_value):
    def one(dim, parts):
        draws = jax.random.uniform(jax.random.fold_in(jax.random.fold_in(rng, 6), dim), (parts,), jnp.float32, smallest / len(pieces), top_value / len(pieces))
        return jnp.repeat(jnp.exp(draws), dims[dim] // parts).reshape((-1,) + (1,) * (len(dims) - dim - 1))

    loudness = one(*pieces[0])
    for cut in pieces[1:]:
        loudness = loudness * one(*cut)
    return loudness


def setup_inputs(seed: int = 0) -> dict:
    arg_keys = jax.random.split(jax.random.key(seed), 9)
    return {
        "species": jnp.clip(jnp.exp(math.log(4.0) - 2.7725887 * jax.random.uniform(arg_keys[0], (NX, NY, NZ, S), jnp.float32) ** steps_of(arg_keys[0], (NX, NY, NZ, S), ((0, 4), (1, 2), (2, 4)), -0.2, 0.2)), 0.25, 4.0),
        "substeps": draw_substeps(jax.random.fold_in(arg_keys[8], 71), 0),
        "reactants": draw_reactants(jax.random.fold_in(arg_keys[8], 71), 0),
        "products": draw_products(jax.random.fold_in(arg_keys[8], 71), 0),
        "rate_const": jnp.clip(jnp.exp(jax.random.uniform(arg_keys[4], (R,), jnp.float32, math.log(0.01), math.log(0.2))), 0.01, 0.2),
        "velocity": jnp.clip(jax.random.uniform(arg_keys[5], (3, NX, NY, NZ), jnp.float32, -0.3, 0.3) * steps_of(arg_keys[5], (3, NX, NY, NZ), ((1, 4), (2, 2), (3, 4)), -0.4, 0.0), -0.3, 0.3),
        "viscosity": jnp.clip(jnp.exp(math.log(1.0) - 1.3862944 * jax.random.uniform(arg_keys[6], (NX, NY, NZ), jnp.float32) ** steps_of(arg_keys[6], (NX, NY, NZ), ((0, 4), (1, 2), (2, 4)), -0.2, 0.2)), 0.25, 1.0),
        "diffusivity": jnp.clip(jnp.exp(jax.random.uniform(arg_keys[7], (S,), jnp.float32, math.log(0.03), math.log(0.12))), 0.03, 0.12),
    }


def react(conc, length, reactant_table, stoich, rate_const):
    logs = jnp.log(conc)
    expo = lax.dot_general(logs, reactant_table, (((1,), (1,)), ((), ())), precision=lax.Precision.HIGHEST, preferred_element_type=jnp.float32)
    rates = (rate_const * jnp.exp(expo)).astype(jnp.bfloat16)
    terms = jnp.dot(rates, stoich, preferred_element_type=jnp.float32)
    width = conc.shape[1]
    made = terms[:, :width]
    used = terms[:, width:]
    return conc * (conc + length * made) / (conc + length * used)


def window(array, axis, offset):
    index = []
    for place in range(3):
        shift = offset if place == axis else 0
        index.append(slice(1 + shift, array.shape[place] - 1 + shift))
    return array[tuple(index)]


def divergence(field, coef, diffusivity):
    inner = window(field, 0, 0)
    visc = window(coef[3], 0, 0)
    total = jnp.zeros(inner.shape, jnp.float32)
    for axis in range(3):
        ahead = window(field, axis, 1)
        behind = window(field, axis, -1)
        speed = window(coef[axis], 0, 0)[..., None]
        speed_behind = window(coef[axis], axis, -1)[..., None]
        visc_ahead = window(coef[3], axis, 1)
        visc_behind = window(coef[3], axis, -1)
        flux_up = speed * (inner + ahead) * 0.5 - diffusivity * ((visc + visc_ahead) * 0.5)[..., None] * (ahead - inner)
        flux_down = speed_behind * (behind + inner) * 0.5 - diffusivity * ((visc_behind + visc) * 0.5)[..., None] * (inner - behind)
        total = total - (flux_up - flux_down)
    return total


def reference(species, substeps, reactants, products, rate_const, velocity, viscosity, diffusivity):
    reactant_table = reactants.astype(jnp.float32)
    stoich = jnp.concatenate([products, reactants], axis=1).astype(jnp.bfloat16)
    cell_counts = jnp.repeat(jnp.repeat(jnp.repeat(substeps, PLANES, axis=0), BY, axis=1), BZ, axis=2)
    rows = species.reshape(-1, BLOCK, S)
    counts = cell_counts.reshape(-1, BLOCK)

    def one_block(pair):
        conc, block_counts = pair
        length = 1.0 / block_counts.astype(jnp.float32)[:, None]
        for level in range(1, MAX_SUB + 1):
            fresh = react(conc, length, reactant_table, stoich, rate_const)
            conc = jnp.where((block_counts >= level)[:, None], fresh, conc)
        return conc

    reacted = lax.map(one_block, (rows, counts)).reshape(NX, NY, NZ, S)
    coef = jnp.concatenate([velocity, viscosity[None]], axis=0)
    coef_pad = jnp.pad(coef, ((0, 0), (1, 1), (1, 1), (1, 1)), mode="wrap")

    def operate(field, diff_group):
        padded = jnp.pad(field, ((1, 1), (1, 1), (1, 1), (0, 0)), mode="wrap")
        return divergence(padded, coef_pad, diff_group)

    def heun(pair):
        field, diff_group = pair
        first = field + operate(field, diff_group)
        return 0.5 * field + 0.5 * (first + operate(first, diff_group))

    grouped = jnp.moveaxis(reacted.reshape(NX, NY, NZ, 8, S // 8), 3, 0)
    diff_groups = diffusivity.reshape(8, S // 8)
    result = lax.map(heun, (grouped, diff_groups))
    return jnp.moveaxis(result, 0, 3).reshape(NX, NY, NZ, S)
```

```python
import functools

import jax
import jax.numpy as jnp
from jax import lax
from jax.experimental import pallas as pl
from jax.experimental.pallas import tpu as pltpu
from jax.sharding import PartitionSpec as P

BLOCK = 128
LOG2E = 1.4426950408889634
SLOT = 16
F32 = jnp.float32
BF16 = jnp.bfloat16
EXACT = lax.Precision.HIGHEST


def lanes_of(shape):
    return lax.broadcasted_iota(jnp.int32, shape, 1)


def rows_of(shape):
    return lax.broadcasted_iota(jnp.int32, shape, 0)


def roll_lanes(tile, shift):
    width = tile.shape[1]
    return pltpu.roll(tile, shift % width, 1)


def pack_x_kernel(species, counts, velocity, viscosity, low, high, table, rows, sem):
    nx, ny, nz = viscosity.shape
    face = low.shape[0] - nz
    cells = nx * ny * nz
    first = pltpu.make_async_copy(species.at[pl.ds(0, face)], low.at[pl.ds(0, face)], sem.at[0])
    last = pltpu.make_async_copy(species.at[pl.ds(cells - face, face)], high.at[pl.ds(0, face)], sem.at[1])
    first.start()
    last.start()
    rows[...] = jnp.zeros_like(rows)
    for x in range(nx):
        for c in range(4):
            part = velocity[c, x] if c < 3 else viscosity[x]
            rows[pl.ds(x * 128 + c * SLOT + 2, ny), :] = part
    eye = (rows_of((nz, nz)) == lanes_of((nz, nz))).astype(F32)
    tiles = lax.dot_general(eye, rows[...], (((1,), (1,)), ((), ())), precision=EXACT, preferred_element_type=F32)
    for x in range(nx):
        table[pl.ds(x * nz, nz), :] = tiles[:, x * 128 : (x + 1) * 128]
    spare = lanes_of((nz, 256)) % 128 >= 4 * SLOT
    blocks = counts.shape[0]
    low[pl.ds(face, nz), :] = jnp.where(spare, counts[0].astype(F32), tiles[:, :256])
    high[pl.ds(face, nz), :] = jnp.where(spare, counts[blocks - 1].astype(F32), tiles[:, nx * 128 - 256 :])
    first.wait()
    last.wait()


def react(conc, length, w_in, w_out, rate):
    logs = jnp.log(conc) * LOG2E
    coarse = logs.astype(BF16)
    fine = (logs - coarse.astype(F32)).astype(BF16)
    count = conc.shape[0]
    both = jnp.concatenate([coarse, fine], axis=0)
    expo = lax.dot_general(both, w_in, (((1,), (1,)), ((), ())), preferred_element_type=F32)
    expo = expo[:count] + expo[count:]
    rates = (rate * jnp.exp2(expo)).astype(BF16)
    terms = jnp.dot(rates, w_out, preferred_element_type=F32)
    width = conc.shape[1]
    return conc * (conc + length * terms[:, :width]) / (conc + length * terms[:, width:])


def react_pair(state, starts, counts, w_in, w_out, rate):
    second = rows_of((2 * BLOCK, 1)) >= BLOCK
    length = jnp.where(second, 1.0 / counts[1].astype(F32), 1.0 / counts[0].astype(F32))
    steps = jnp.where(second, counts[1], counts[0])

    def level(number, carry):
        conc = jnp.concatenate([state[pl.ds(start, BLOCK), :] for start in starts], axis=0)
        fresh = react(conc, length, w_in[...], w_out[...], rate[...])
        fresh = jnp.where(number < steps, fresh, conc)
        for place, start in enumerate(starts):
            state[pl.ds(start, BLOCK), :] = fresh[place * BLOCK : (place + 1) * BLOCK]
        return carry

    lax.fori_loop(0, jnp.maximum(counts[0], counts[1]), level, 0)


def chemistry_kernel(counts, species, reactants, products, rate, field, w_in, w_out):
    w_in[...] = reactants[...].astype(F32).astype(BF16)
    width = species.shape[1]
    w_out[:, :width] = products[...].astype(F32).astype(BF16)
    w_out[:, width:] = reactants[...].astype(F32).astype(BF16)
    field[...] = species[...]
    blocks = counts.shape[0]
    keys = [counts[b] * blocks + b for b in range(blocks)]
    for end in range(blocks - 1, 0, -1):
        for i in range(end):
            keys[i], keys[i + 1] = jnp.maximum(keys[i], keys[i + 1]), jnp.minimum(keys[i], keys[i + 1])
    for i in range(0, blocks, 2):
        starts = [pl.multiple_of((k % blocks) * BLOCK, BLOCK) for k in keys[i : i + 2]]
        react_pair(field, starts, [k // blocks for k in keys[i : i + 2]], w_in, w_out, rate)


def shifted_slots(tile, shift, keep):
    slot = lanes_of(tile.shape) % SLOT
    hit = (slot == keep[0]) | (slot == keep[1])
    return jnp.where(hit, roll_lanes(tile, shift), 0.0)


def pack_yz_kernel(dims, before, after, field, table, w_in, w_out, rate, halo, tiles, ymsg, zlow, zhigh, yzlow, yzhigh, split):
    nx, ny, nz = dims
    face = 2 * ny * nz
    plane = ny * nz
    halo[pl.ds(0, face), :] = before[pl.ds(0, face), :]
    halo[pl.ds(face, face), :] = after[pl.ds(0, face), :]
    counts = [jnp.max(side[pl.ds(face, 8), pl.ds(128, 128)][:, 64:]).astype(jnp.int32) for side in (before, after)]
    react_pair(halo, [0, face], counts, w_in, w_out, rate)

    used = lanes_of((nz, 128)) < 4 * SLOT
    tiles[...] = jnp.zeros_like(tiles)
    for k in range(2):
        half = pl.ds(128 * k, 128)
        tiles[pl.ds(k * nz, nz), :] = jnp.where(used, before[pl.ds(face, nz), half], 0.0)
        tiles[pl.ds((nx + 2 + k) * nz, nz), :] = jnp.where(used, after[pl.ds(face, nz), half], 0.0)
    tiles[pl.ds(2 * nz, nx * nz), :] = table[...]

    def column(x, y):
        if x < 0:
            return halo[pl.ds((x + 2) * plane + y * nz, nz), :]
        if x >= nx:
            return halo[pl.ds(face + (x - nx) * plane + y * nz, nz), :]
        return field[pl.ds(x * plane + y * nz, nz), :]

    for side, near, far, shift, keep in ((0, 0, 1, ny, (ny + 2, ny + 3)), (1, ny - 1, ny - 2, -ny, (0, 1))):
        row = 0
        for x in range(-1, nx + 1):
            ymsg[side, pl.ds(row, nz), :] = column(x, near)
            row += nz
        for x in range(nx):
            ymsg[side, pl.ds(row, nz), :] = column(x, far)
            row += nz
        for x in range(nx + 4):
            moved = shifted_slots(tiles[pl.ds(x * nz, nz), :], shift, keep)
            ymsg[side, pl.ds(row + (x // 2) * nz, nz), pl.ds((x % 2) * 128, 128)] = moved

    cells = nx * plane
    total = cells + 2 * plane
    halves = [pl.ds(128 * k, 128) for k in range(field.shape[1] // 128)]
    for k, half in enumerate(halves):
        split[pl.ds(k * total, cells), :] = field[:, half]
        split[pl.ds(k * total + cells, plane), :] = halo[pl.ds(plane, plane), half]
        split[pl.ds(k * total + cells + plane, plane), :] = halo[pl.ds(face, plane), half]

    for msg, edge, near, far, slots in ((zlow, yzlow, 0, 1, (0, 1)), (zhigh, yzhigh, nz - 1, nz - 2, (nz - 2, nz - 1))):
        columns = nx * ny
        for k, half in enumerate(halves):
            base = k * total
            msg[pl.ds(0, columns), half] = split[pl.ds(base + near, columns, stride=nz), :]
            msg[pl.ds(columns, columns), half] = split[pl.ds(base + far, columns, stride=nz), :]
            msg[pl.ds(2 * columns, 2 * ny), half] = split[pl.ds(base + cells + near, 2 * ny, stride=nz), :]
        row = 2 * columns + 2 * ny
        coarse = [tiles[pl.ds(z, 16, stride=nz), :] for z in slots]
        for k in range(2):
            msg[pl.ds(row, 16), pl.ds(128 * k, 128)] = coarse[k]
        for side, y, shift, keep in ((0, 0, ny, (ny + 2, ny + 3)), (1, ny - 1, -ny, (0, 1))):
            for k, half in enumerate(halves):
                edge[side, pl.ds(0, nx), half] = split[pl.ds(k * total + y * nz + near, nx, stride=plane), :]
            for k in range(2):
                edge[side, pl.ds(nx, 16), pl.ds(128 * k, 128)] = shifted_slots(coarse[k], shift, keep)


def ring_up(main, rest):
    count = main.shape[0]
    last = rows_of(main.shape) == count - 1
    a, b = pltpu.roll(main, count - 1, 0), pltpu.roll(rest, count - 1, 0)
    return jnp.where(last, b, a), jnp.where(last, a, b)


def ring_down(main, rest):
    zero = rows_of(main.shape) == 0
    a, b = pltpu.roll(main, 1, 0), pltpu.roll(rest, 1, 0)
    return jnp.where(zero, b, a), jnp.where(zero, a, b)


UX, UY, UZ, UZ_DOWN, QX, QY, QZ, QZ_DOWN = range(8)


def transport_kernel(
    dims, field, halo, tiles, ymsg, zbefore, zafter, yzbefore, yzafter, diffusivity, out, rest, main_tiles, rest_tiles, first, first_rest
):
    nx, ny, nz = dims
    plane, face, columns = ny * nz, 2 * ny * nz, nx * ny
    yrow = (2 * nx + 2) * nz
    halves = [pl.ds(128 * k, 128) for k in range(field.shape[1] // 128)]
    rest_rows = rest.shape[0] // len(halves)

    def rest_column(x, y):
        if y == -1:
            return columns + 2 * ny + x
        if y == ny:
            return columns + 2 * ny + nx + x
        if x == -1:
            return columns + y
        if x == nx:
            return columns + ny + y
        return x * ny + y

    for msg, edge, near, far in ((zafter, yzafter, 0, 1), (zbefore, yzbefore, nz - 1, nz - 2)):
        for k, half in enumerate(halves):
            base = k * rest_rows
            rest[pl.ds(base + near, columns, stride=nz), :] = msg[pl.ds(0, columns), half]
            rest[pl.ds(base + far, columns, stride=nz), :] = msg[pl.ds(columns, columns), half]
            base += columns * nz
            rest[pl.ds(base + near, 2 * ny, stride=nz), :] = msg[pl.ds(2 * columns, 2 * ny), half]
            base += 2 * ny * nz
            rest[pl.ds(base + near, nx, stride=nz), :] = edge[1, pl.ds(0, nx), half]
            rest[pl.ds(base + nx * nz + near, nx, stride=nz), :] = edge[0, pl.ds(0, nx), half]

    rest_tiles[...] = jnp.zeros_like(rest_tiles)
    row = 2 * columns + 2 * ny
    for msg, edge, slots in ((zafter, yzafter, (0, 1)), (zbefore, yzbefore, (nz - 2, nz - 1))):
        for k, z in enumerate(slots):
            half = pl.ds(128 * k, 128)
            total = msg[pl.ds(row, 16), half] + edge[0, pl.ds(nx, 16), half] + edge[1, pl.ds(nx, 16), half]
            rest_tiles[pl.ds(z, 16, stride=nz), :] = total
    for x in range(nx + 4):
        half = pl.ds((x % 2) * 128, 128)
        spot = pl.ds(yrow + (x // 2) * nz, nz)
        main_tiles[pl.ds(x * nz, nz), :] = tiles[pl.ds(x * nz, nz), :] + ymsg[0, spot, half] + ymsg[1, spot, half]

    group = lanes_of((nz, 128)) // SLOT

    def place(tile, source, target):
        return jnp.where(group == target, roll_lanes(tile, (target - source) * SLOT), 0.0)

    for x in range(nx + 3):
        spot, nxt = pl.ds(x * nz, nz), pl.ds((x + 1) * nz, nz)
        raw = (main_tiles[spot, :], rest_tiles[spot, :])
        ahead = (main_tiles[nxt, :], rest_tiles[nxt, :])
        above = ring_up(*raw)
        qz = tuple(a + b for a, b in zip(raw, above))
        qz_down = ring_down(*qz)
        down = ring_down(*raw)
        for k, ref in enumerate((main_tiles, rest_tiles)):
            tile = jnp.where(group < 3, raw[k], 0.0)
            tile += place(down[k], 2, UZ_DOWN)
            tile += place(raw[k] + ahead[k], 3, QX)
            tile += place(raw[k] + roll_lanes(raw[k], -1), 3, QY)
            tile += place(qz[k], 3, QZ)
            tile += place(qz_down[k], 3, QZ_DOWN)
            ref[spot, :] = 0.5 * tile

    diff = diffusivity[...]

    def coefficients(ref, x, y):
        here = ref[pl.ds((x + 2) * nz, nz), :]
        behind = ref[pl.ds((x + 1) * nz, nz), :]

        def pick(tile, kind, y):
            lane = kind * SLOT + y + 2
            return tile[:, lane : lane + 1]

        return (
            (pick(here, UX, y), pick(here, QX, y), pick(behind, UX, y), pick(behind, QX, y)),
            (pick(here, UY, y), pick(here, QY, y), pick(here, UY, y - 1), pick(here, QY, y - 1)),
            (pick(here, UZ, y), pick(here, QZ, y), pick(here, UZ_DOWN, y), pick(here, QZ_DOWN, y)),
        )

    def change(coef, value, pairs):
        flow = jnp.zeros_like(value)
        spread = jnp.zeros_like(value)
        for (u, q, u_down, q_down), (ahead, behind) in zip(coef, pairs):
            flow += u_down * (value + behind) - u * (value + ahead)
            spread += q * (ahead - value) + q_down * (behind - value)
        return flow + diff * spread

    def main(x, y):
        if y in (-1, ny):
            return ymsg[1 if y < 0 else 0, pl.ds((x + 1) * nz, nz), :]
        if y in (-2, ny + 1):
            return ymsg[1 if y < 0 else 0, pl.ds((nx + 2 + x) * nz, nz), :]
        if x < 0:
            return halo[pl.ds((x + 2) * plane + y * nz, nz), :]
        if x >= nx:
            return halo[pl.ds(face + (x - nx) * plane + y * nz, nz), :]
        return field[pl.ds(x * plane + y * nz, nz), :]

    def remainder(x, y):
        row = rest_column(x, y) * nz
        parts = [rest[pl.ds(k * rest_rows + row, nz), :] for k in range(len(halves))]
        return jnp.concatenate(parts, axis=1)

    inside = [(x, y) for x in range(nx) for y in range(ny)]
    ends = [(x, y) for x in (-1, nx) for y in range(ny)] + [(x, y) for y in (-1, ny) for x in range(nx)]
    for x, y in inside + ends:
        value, other = main(x, y), remainder(x, y)
        up, down = ring_up(value, other), ring_down(value, other)
        pairs = ((main(x + 1, y), main(x - 1, y)), (main(x, y + 1), main(x, y - 1)), (up[0], down[0]))
        new = value + change(coefficients(main_tiles, x, y), value, pairs)
        first[pl.ds(rest_column(x, y) * nz, nz), :] = new
        if (x, y) in inside:
            pairs = (
                (remainder(x + 1, y), remainder(x - 1, y)),
                (remainder(x, y + 1), remainder(x, y - 1)),
                (up[1], down[1]),
            )
            new = other + change(coefficients(rest_tiles, x, y), other, pairs)
            first_rest[pl.ds(rest_column(x, y) * nz, nz), :] = new

    def stage(x, y):
        return first[pl.ds(rest_column(x, y) * nz, nz), :]

    for x, y in inside:
        value, other = stage(x, y), first_rest[pl.ds(rest_column(x, y) * nz, nz), :]
        up, down = ring_up(value, other), ring_down(value, other)
        pairs = ((stage(x + 1, y), stage(x - 1, y)), (stage(x, y + 1), stage(x, y - 1)), (up[0], down[0]))
        new = value + change(coefficients(main_tiles, x, y), value, pairs)
        out[pl.ds(x * plane + y * nz, nz), :] = 0.5 * (main(x, y) + new)


def hop(axis, step):
    peers = lax.axis_size(axis)
    return [(i, (i + step) % peers) for i in range(peers)]


def hop2(axes, steps):
    a, b = (lax.axis_size(axis) for axis in axes)
    return [
        (i * b + j, ((i + steps[0]) % a) * b + (j + steps[1]) % b) for i in range(a) for j in range(b)
    ]


def shards(species, substeps, reactants, products, rate_const, velocity, viscosity, diffusivity):
    nx, ny, nz, width = species.shape
    dims = (nx, ny, nz)
    cells, columns, face = nx * ny * nz, nx * ny, 2 * ny * nz
    reactions = reactants.shape[0]
    vmem = pl.BlockSpec(memory_space=pltpu.VMEM)
    smem = pl.BlockSpec(memory_space=pltpu.SMEM)
    anyspace = pl.BlockSpec(memory_space=pl.ANY)
    rows = species.reshape(cells, width)
    counts = substeps.reshape(-1)
    rate = rate_const.reshape(1, reactions)
    shape = lambda *dims: jax.ShapeDtypeStruct(dims, F32)

    low, high, table = pl.pallas_call(
        pack_x_kernel,
        out_shape=(shape(face + nz, width), shape(face + nz, width), shape(nx * nz, 128)),
        in_specs=[anyspace, smem, vmem, vmem],
        out_specs=(vmem, vmem, vmem),
        scratch_shapes=[pltpu.VMEM((nx * 128, nz), F32), pltpu.SemaphoreType.DMA((2,))],
        name="pack_x",
    )(rows, counts, velocity, viscosity)
    before = lax.ppermute(high, "gx", hop("gx", 1))
    after = lax.ppermute(low, "gx", hop("gx", -1))

    field, w_in, w_out = pl.pallas_call(
        chemistry_kernel,
        out_shape=(
            shape(cells, width),
            jax.ShapeDtypeStruct((reactions, width), BF16),
            jax.ShapeDtypeStruct((reactions, 2 * width), BF16),
        ),
        in_specs=[smem, vmem, vmem, vmem, vmem],
        out_specs=(vmem, vmem, vmem),
        name="chemistry",
    )(counts, rows, reactants, products, rate)

    yrows = (2 * nx + 2) * nz + (nx + 4) // 2 * nz
    zrows = 2 * columns + 2 * ny + 16
    halo, tiles, ymsg, zlow, zhigh, yzlow, yzhigh = pl.pallas_call(
        functools.partial(pack_yz_kernel, dims),
        out_shape=(
            shape(2 * face, width),
            shape(16 * nz, 128),
            shape(2, yrows, width),
            shape(zrows, width),
            shape(zrows, width),
            shape(2, nx + 16, width),
            shape(2, nx + 16, width),
        ),
        in_specs=[vmem] * 7,
        out_specs=(vmem,) * 7,
        scratch_shapes=[pltpu.VMEM((width // 128 * (nx + 2) * ny * nz, 128), F32)],
        name="pack_yz",
    )(before, after, field, table, w_in, w_out, rate)

    zbefore = lax.ppermute(zhigh, "gz", hop("gz", 1))
    zafter = lax.ppermute(zlow, "gz", hop("gz", -1))
    if lax.axis_size("gy") == 2:
        yrecv = lax.ppermute(ymsg, "gy", hop("gy", 1))
        yzbefore = lax.ppermute(yzhigh, ("gy", "gz"), hop2(("gy", "gz"), (1, 1)))
        yzafter = lax.ppermute(yzlow, ("gy", "gz"), hop2(("gy", "gz"), (1, -1)))
    else:
        yrecv = jnp.stack([lax.ppermute(ymsg[side], "gy", hop("gy", step)) for side, step in ((0, -1), (1, 1))])
        yzbefore, yzafter = (
            jnp.stack(
                [
                    lax.ppermute(msg[side], ("gy", "gz"), hop2(("gy", "gz"), (step, zstep)))
                    for side, step in ((0, -1), (1, 1))
                ]
            )
            for msg, zstep in ((yzhigh, 1), (yzlow, -1))
        )

    rest_rows = (columns + 2 * ny + 2 * nx) * nz
    out = pl.pallas_call(
        functools.partial(transport_kernel, dims),
        out_shape=shape(cells, width),
        in_specs=[vmem] * 9,
        out_specs=vmem,
        scratch_shapes=[
            pltpu.VMEM((width // 128 * rest_rows, 128), F32),
            pltpu.VMEM((16 * nz, 128), F32),
            pltpu.VMEM((16 * nz, 128), F32),
            pltpu.VMEM((rest_rows, width), F32),
            pltpu.VMEM((columns * nz, width), F32),
        ],
        name="transport",
    )(field, halo, tiles, yrecv, zbefore, zafter, yzbefore, yzafter, diffusivity.reshape(1, width))
    return out.reshape(nx, ny, nz, width)


def solution(mesh):
    return jax.shard_map(
        shards,
        mesh=mesh,
        in_specs=(
            P("gx", "gy", "gz", None),
            P("gx", "gy", "gz"),
            P(),
            P(),
            P(),
            P(None, "gx", "gy", "gz"),
            P("gx", "gy", "gz"),
            P(),
        ),
        out_specs=P("gx", "gy", "gz", None),
        check_vma=False,
    )
```

```python
import functools

import jax
import jax.numpy as jnp
from jax import lax
from jax.experimental import pallas as pl
from jax.experimental.pallas import tpu as pltpu
from jax.sharding import PartitionSpec as P

BLOCK = 128
LOG2E = 1.4426950408889634
SLOT = 16
F32 = jnp.float32
BF16 = jnp.bfloat16
EXACT = lax.Precision.HIGHEST


def lanes_of(shape):
    return lax.broadcasted_iota(jnp.int32, shape, 1)


def rows_of(shape):
    return lax.broadcasted_iota(jnp.int32, shape, 0)


def roll_lanes(tile, shift):
    width = tile.shape[1]
    return pltpu.roll(tile, shift % width, 1)


def pack_x_kernel(
    species, counts, velocity, viscosity, reactants, products, rate, diffusivity,
    low, high, table, rows, reactants_out, products_out, rate_out, diff_out,
    padded, speeds, drag, steps, sem,
):
    nx, ny, nz = drag.shape
    face = low.shape[0] - nz
    cells = nx * ny * nz
    moves = ((velocity, speeds), (viscosity, drag), (counts, steps), (species, rows), (reactants, reactants_out),
             (products, products_out), (rate, rate_out), (diffusivity, diff_out))
    copies = [pltpu.make_async_copy(source, target, sem.at[k]) for k, (source, target) in enumerate(moves)]
    for copy in copies:
        copy.start()
    padded[...] = jnp.zeros_like(padded)
    for copy in copies[:3]:
        copy.wait()
    for x in range(nx):
        for c in range(4):
            part = speeds[c, x] if c < 3 else drag[x]
            padded[pl.ds(x * 128 + c * SLOT + 2, ny), :] = part
    eye = (rows_of((nz, nz)) == lanes_of((nz, nz))).astype(F32)
    tiles = lax.dot_general(eye, padded[...], (((1,), (1,)), ((), ())), precision=EXACT, preferred_element_type=F32)
    for x in range(nx):
        table[pl.ds(x * nz, nz), :] = tiles[:, x * 128 : (x + 1) * 128]
    spare = lanes_of((nz, 256)) % 128 >= 4 * SLOT
    blocks = steps.shape[0]
    low[pl.ds(face, nz), :] = jnp.where(spare, steps[0].astype(F32), tiles[:, :256])
    high[pl.ds(face, nz), :] = jnp.where(spare, steps[blocks - 1].astype(F32), tiles[:, nx * 128 - 256 :])
    copies[3].wait()
    low[pl.ds(0, face), :] = rows[pl.ds(0, face), :]
    high[pl.ds(0, face), :] = rows[pl.ds(cells - face, face), :]
    for copy in copies[4:]:
        copy.wait()


def react(conc, length, w_in, w_out, rate):
    logs = jnp.log(conc) * LOG2E
    coarse = logs.astype(BF16)
    fine = (logs - coarse.astype(F32)).astype(BF16)
    both = jnp.concatenate([coarse, fine], axis=0)
    expo = jnp.dot(w_in, both, preferred_element_type=F32)
    rates = (jnp.concatenate([rate, rate], axis=1) * jnp.exp2(expo)).astype(BF16)
    terms = jnp.dot(w_out, rates, preferred_element_type=F32)
    width = conc.shape[0]
    return conc * (conc + length * terms[:width]) / (conc + length * terms[width:])


def react_pair(state, places, counts, number, tables):
    second = lanes_of((1, 2 * BLOCK)) >= BLOCK
    length = jnp.where(second, 1.0 / counts[1].astype(F32), 1.0 / counts[0].astype(F32))
    steps = jnp.where(second, counts[1], counts[0])
    conc = jnp.concatenate([state[place] for place in places], axis=1)
    fresh = react(conc, length, *(table[...] for table in tables))
    fresh = jnp.where(number < steps, fresh, conc)
    return [fresh[:, k * BLOCK : (k + 1) * BLOCK] for k in range(2)]


def run_levels(state, first, last, groups, tables):
    def level(number, carry):
        fresh = [react_pair(state, places, counts, number + offset, tables) for places, counts, offset in groups]
        for (places, _, _), values in zip(groups, fresh):
            for place, value in zip(places, values):
                state[place] = value
        return carry

    lax.fori_loop(first, last, level, 0)


def ranked(counts):
    blocks = counts.shape[0]
    keys = [counts[b] * blocks + b for b in range(blocks)]
    for end in range(blocks - 1, 0, -1):
        for i in range(end):
            keys[i], keys[i + 1] = jnp.maximum(keys[i], keys[i + 1]), jnp.minimum(keys[i], keys[i + 1])
    return [k % blocks for k in keys], [k // blocks for k in keys]


def chemistry_kernel(counts, species, reactants, products, rate_row, field, w_in, w_out, rate, state, steps, sem):
    copy = pltpu.make_async_copy(counts, steps, sem)
    copy.start()
    width = species.shape[1]
    reactions = reactants.shape[0]
    table = reactants[...].astype(F32)
    w_in[:, :width] = table.astype(BF16)
    w_in[:, width:] = table.astype(BF16)
    w_out[:width, :] = products[...].astype(F32).T.astype(BF16)
    w_out[width:, :] = table.T.astype(BF16)
    rate[...] = jnp.broadcast_to(rate_row[...], (128, reactions)).T
    for b in range(steps.shape[0]):
        state[b] = species[pl.ds(b * BLOCK, BLOCK), :].T
    copy.wait()
    places, numbers = ranked(steps)
    groups = [(places[:2], numbers[:2], 0), (places[2:], numbers[2:], 0)]
    run_levels(state, 0, numbers[2], groups, (w_in, w_out, rate))
    run_levels(state, numbers[2], numbers[0], groups[:1], (w_in, w_out, rate))
    for b in range(steps.shape[0]):
        field[pl.ds(b * BLOCK, BLOCK), :] = state[b].T


def shifted_slots(tile, shift, keep):
    slot = lanes_of(tile.shape) % SLOT
    hit = (slot == keep[0]) | (slot == keep[1])
    return jnp.where(hit, roll_lanes(tile, shift), 0.0)


def pack_yz_kernel(
    dims, before, after, field, table, w_in, w_out, rate,
    halo, tiles, ymsg, zlow, zhigh, yzlow, yzhigh,
    split, state,
):
    nx, ny, nz = dims
    face = 2 * ny * nz
    plane = ny * nz
    for k, side in enumerate((before, after)):
        state[k] = side[pl.ds(0, face), :].T
    ends = [jnp.max(side[pl.ds(face, 8), pl.ds(128, 128)][:, 64:]).astype(jnp.int32) for side in (before, after)]
    run_levels(state, 0, jnp.maximum(ends[0], ends[1]), [([0, 1], ends, 0)], (w_in, w_out, rate))
    for k in range(2):
        halo[pl.ds(k * face, face), :] = state[k].T

    used = lanes_of((nz, 128)) < 4 * SLOT
    tiles[...] = jnp.zeros_like(tiles)
    for k in range(2):
        half = pl.ds(128 * k, 128)
        tiles[pl.ds(k * nz, nz), :] = jnp.where(used, before[pl.ds(face, nz), half], 0.0)
        tiles[pl.ds((nx + 2 + k) * nz, nz), :] = jnp.where(used, after[pl.ds(face, nz), half], 0.0)
    tiles[pl.ds(2 * nz, nx * nz), :] = table[...]

    def column(x, y):
        if x < 0:
            return halo[pl.ds((x + 2) * plane + y * nz, nz), :]
        if x >= nx:
            return halo[pl.ds(face + (x - nx) * plane + y * nz, nz), :]
        return field[pl.ds(x * plane + y * nz, nz), :]

    for side, near, far, shift, keep in ((0, 0, 1, ny, (ny + 2, ny + 3)), (1, ny - 1, ny - 2, -ny, (0, 1))):
        row = 0
        for x in range(-1, nx + 1):
            ymsg[side, pl.ds(row, nz), :] = column(x, near)
            row += nz
        for x in range(nx):
            ymsg[side, pl.ds(row, nz), :] = column(x, far)
            row += nz
        for x in range(nx + 4):
            moved = shifted_slots(tiles[pl.ds(x * nz, nz), :], shift, keep)
            ymsg[side, pl.ds(row + (x // 2) * nz, nz), pl.ds((x % 2) * 128, 128)] = moved

    cells = nx * plane
    total = cells + 2 * plane
    halves = [pl.ds(128 * k, 128) for k in range(field.shape[1] // 128)]
    for k, half in enumerate(halves):
        split[pl.ds(k * total, cells), :] = field[:, half]
        split[pl.ds(k * total + cells, plane), :] = halo[pl.ds(plane, plane), half]
        split[pl.ds(k * total + cells + plane, plane), :] = halo[pl.ds(face, plane), half]

    for msg, edge, near, far, slots in ((zlow, yzlow, 0, 1, (0, 1)), (zhigh, yzhigh, nz - 1, nz - 2, (nz - 2, nz - 1))):
        columns = nx * ny
        for k, half in enumerate(halves):
            base = k * total
            msg[pl.ds(0, columns), half] = split[pl.ds(base + near, columns, stride=nz), :]
            msg[pl.ds(columns, columns), half] = split[pl.ds(base + far, columns, stride=nz), :]
            msg[pl.ds(2 * columns, 2 * ny), half] = split[pl.ds(base + cells + near, 2 * ny, stride=nz), :]
        row = 2 * columns + 2 * ny
        coarse = [tiles[pl.ds(z, 16, stride=nz), :] for z in slots]
        for k in range(2):
            msg[pl.ds(row, 16), pl.ds(128 * k, 128)] = coarse[k]
        for side, y, shift, keep in ((0, 0, ny, (ny + 2, ny + 3)), (1, ny - 1, -ny, (0, 1))):
            for k, half in enumerate(halves):
                edge[side, pl.ds(0, nx), half] = split[pl.ds(k * total + y * nz + near, nx, stride=plane), :]
            for k in range(2):
                edge[side, pl.ds(nx, 16), pl.ds(128 * k, 128)] = shifted_slots(coarse[k], shift, keep)


UX, UY, UZ, M, UZ_IN, QX, QY, QZ = range(8)


def flux(speed, spread, low, high):
    return speed * (low + high) - spread * (high - low)


def spot(x, y, nz):
    return ((x + 2) * 12 + y + 2) * nz


def picked(tile, kind, y):
    lane = kind * SLOT + y + 2
    return jnp.broadcast_to(0.5 * tile[:, lane : lane + 1], (tile.shape[0], 128))


def interior_z(value, speed, spread):
    count = value.shape[0]
    up = flux(speed, spread, value, pltpu.roll(value, count - 1, 0))
    return pltpu.roll(up, 1, 0) - up


def partial_kernel(dims, field, halo, tiles, diffusivity, coef, part, copy):
    nx, ny, nz = dims
    plane, face = ny * nz, 2 * ny * nz
    halves = [pl.ds(128 * k, 128) for k in range(field.shape[1] // 128)]
    last = rows_of((nz, 128)) == nz - 1

    def main(x, y, half):
        if x < 0:
            return halo[pl.ds((x + 2) * plane + y * nz, nz), half]
        if x >= nx:
            return halo[pl.ds(face + (x - nx) * plane + y * nz, nz), half]
        return field[pl.ds(x * plane + y * nz, nz), half]

    for x in range(-2, nx + 2):
        tile = tiles[pl.ds((x + 2) * nz, nz), :]
        for y in range(ny):
            row = pl.ds(spot(x, y, nz), nz)
            drag = picked(tile, M, y)
            coef[M, row, :] = drag
            if x <= nx:
                coef[UX, row, :] = picked(tile, UX, y)
            if -1 <= x <= nx:
                coef[UY, row, :] = picked(tile, UY, y)
                speed = picked(tile, UZ, y)
                coef[UZ, row, :] = speed
                coef[UZ_IN, row, :] = jnp.where(last, 0.0, speed)
                coef[QZ, row, :] = jnp.where(last, 0.0, drag + pltpu.roll(drag, nz - 1, 0))
                if y:
                    coef[QY, pl.ds(spot(x, y - 1, nz), nz), :] = drag + coef[M, pl.ds(spot(x, y - 1, nz), nz), :]
            if x > -2:
                coef[QX, pl.ds(spot(x - 1, y, nz), nz), :] = drag + coef[M, pl.ds(spot(x - 1, y, nz), nz), :]

    def at(kind, x, y):
        return coef[kind, pl.ds(spot(x, y, nz), nz), :]

    for k, half in enumerate(halves):
        diff = jnp.broadcast_to(diffusivity[:, half], (nz, 128))
        behind = [flux(at(UX, -2, y), diff * at(QX, -2, y), main(-2, y, half), main(-1, y, half)) for y in range(ny)]
        for x in range(-1, nx + 1):
            below = None
            for y in range(ny):
                value = main(x, y, half)
                ahead = flux(at(UX, x, y), diff * at(QX, x, y), value, main(x + 1, y, half))
                total = value + (behind[y] - ahead)
                behind[y] = ahead
                if below is not None:
                    total += below
                if y < ny - 1:
                    below = flux(at(UY, x, y), diff * at(QY, x, y), value, main(x, y + 1, half))
                    total -= below
                total += interior_z(value, at(UZ_IN, x, y), diff * at(QZ, x, y))
                row = pl.ds(((x + 1) * ny + y) * nz, nz)
                part[k, row, :] = total
                copy[k, row, :] = value


def transport_kernel(
    dims, field, tiles, coef, part, copy, ymsg, zbefore, zafter, yzbefore, yzafter, diffusivity, out,
    ring, side, edge, first, edge_copy, zplane, gplane, ends,
):
    nx, ny, nz = dims
    columns, grid = nx * ny, (nx + 2) * ny
    halves = [pl.ds(128 * k, 128) for k in range(field.shape[1] // 128)]
    last = rows_of((nz, 128)) == nz - 1
    zsides = ((zbefore, yzbefore, nz - 1, nz - 2), (zafter, yzafter, 0, 1))
    crow = 2 * columns + 2 * ny
    yrow = (2 * nx + 2) * nz
    high, low = 0, 1

    def tile_of(x):
        place, half = pl.ds(yrow + (x + 2) // 2 * nz, nz), pl.ds((x % 2) * 128, 128)
        return ymsg[0, place, half] + ymsg[1, place, half]

    for x in range(-1, nx + 1):
        tile = tile_of(x)
        inner = 0 <= x < nx
        for y in (-2, -1, ny, ny + 1) if inner else (-1, ny):
            row = pl.ds(spot(x, y, nz), nz)
            drag = picked(tile, M, y)
            side[M, row, :] = drag
            if y in (-2, -1, ny):
                side[UY, row, :] = picked(tile, UY, y)
            if y in (-1, ny):
                if x < nx:
                    side[UX, row, :] = picked(tile, UX, y)
                if x > -1:
                    side[QX, pl.ds(spot(x - 1, y, nz), nz), :] = drag + side[M, pl.ds(spot(x - 1, y, nz), nz), :]
                if inner:
                    speed = picked(tile, UZ, y)
                    side[UZ, row, :] = speed
                    side[UZ_IN, row, :] = jnp.where(last, 0.0, speed)
                    side[QZ, row, :] = jnp.where(last, 0.0, drag + pltpu.roll(drag, nz - 1, 0))
        for y, nxt in ((-1, 0), (ny - 1, ny)):
            total = (side if y < 0 else coef)[M, pl.ds(spot(x, y, nz), nz), :]
            total += (side if nxt == ny else coef)[M, pl.ds(spot(x, nxt, nz), nz), :]
            side[QY, pl.ds(spot(x, y, nz), nz), :] = total
        if inner:
            for y in (-2, ny):
                side[QY, pl.ds(spot(x, y, nz), nz), :] = (
                    side[M, pl.ds(spot(x, y, nz), nz), :] + side[M, pl.ds(spot(x, y + 1, nz), nz), :]
                )

    ring[...] = jnp.zeros_like(ring)
    for msg, corner, near, far in zsides:
        slots = (0, 1) if near == 0 else (nz - 2, nz - 1)
        for k, z in enumerate(slots):
            half = pl.ds(128 * k, 128)
            total = msg[pl.ds(crow, 16), half] + corner[0, pl.ds(nx, 16), half] + corner[1, pl.ds(nx, 16), half]
            ring[pl.ds(z, 16, stride=nz), :] = total

    def ring_row(x, y):
        return ((x + 1) * (ny + 2) + y + 1) * nz

    for x in range(-1, nx + 1):
        tile = ring[pl.ds((x + 2) * nz, nz), :]
        inner = 0 <= x < nx
        for y in range(-1, ny + 1):
            row = pl.ds(ring_row(x, y), nz)
            own = 0 <= y < ny
            if not (inner or own):
                continue
            edge[M, row, :] = picked(tile, M, y)
            edge[UZ, row, :] = picked(tile, UZ, y)
            if own and x < nx:
                edge[UX, row, :] = picked(tile, UX, y)
            if inner and y < ny:
                edge[UY, row, :] = picked(tile, UY, y)

    def at(kind, x, y):
        ref = coef if 0 <= y < ny and not (kind == QY and y == ny - 1) else side
        return ref[kind, pl.ds(spot(x, y, nz), nz), :]

    def beyond(kind, x, y, z):
        return edge[kind, pl.ds(ring_row(x, y) + z, ny, stride=nz), :]

    def end_coefficients(group, near, far):
        x, y = group
        inside = 0 if near == nz - 1 else nz - 1
        if x is None:
            outer = [edge[kind, pl.ds(ring_row(0, y) + near, nx, stride=(ny + 2) * nz), :] for kind in (UZ, M)]
            inner = [side[kind, pl.ds(spot(0, y, nz) + inside, nx, stride=12 * nz), :] for kind in (UZ, M)]
        else:
            outer = [beyond(kind, x, 0, near) for kind in (UZ, M)]
            inner = [coef[kind, pl.ds(spot(x, 0, nz) + inside, ny, stride=nz), :] for kind in (UZ, M)]
        return outer[0] if near == nz - 1 else inner[0], outer[1] + inner[1]

    groups = [(x, None) for x in range(-1, nx + 1)] + [(None, -1), (None, ny)]
    pitch = ny + 2
    for k, half in enumerate(halves):
        diff = jnp.broadcast_to(diffusivity[:, half], (nz, 128))

        def main(x, y):
            if y in (-1, ny):
                return ymsg[low if y < 0 else high, pl.ds((x + 1) * nz, nz), half]
            if y in (-2, ny + 1):
                return ymsg[low if y < 0 else high, pl.ds((nx + 2 + x) * nz, nz), half]
            return copy[k, pl.ds(((x + 1) * ny + y) * nz, nz), :]

        def first_row(x, y):
            if 0 <= y < ny:
                return ((x + 1) * ny + y) * nz
            return (grid + (0 if y < 0 else nx) + x) * nz

        def along(kind, spread, x, y, step):
            return flux(at(kind, x, y), diff * at(spread, x, y), main(x, y), main(x + step[0], y + step[1]))

        behind = {y: along(UX, QX, -1, y, (1, 0)) for y in (-1, ny)}
        for x in range(-1, nx + 1):
            into, outof = along(UY, QY, x, -1, (0, 1)), along(UY, QY, x, ny - 1, (0, 1))
            for y in range(ny):
                row = pl.ds(first_row(x, y), nz)
                total = part[k, row, :]
                if y == 0:
                    total += into
                if y == ny - 1:
                    total -= outof
                first[k, row, :] = total
            if 0 <= x < nx:
                for y in (-1, ny):
                    value = main(x, y)
                    ahead = along(UX, QX, x, y, (1, 0))
                    total = value + (behind[y] - ahead)
                    behind[y] = ahead
                    if y < 0:
                        total += along(UY, QY, x, -2, (0, 1)) - into
                    else:
                        total += outof - along(UY, QY, x, ny, (0, 1))
                    total += interior_z(value, at(UZ_IN, x, y), diff * at(QZ, x, y))
                    first[k, pl.ds(first_row(x, y), nz), :] = total
                    edge_copy[k, pl.ds(first_row(x, y) - grid * nz, nz), :] = value

        for number, (msg, corner, near, far) in enumerate(zsides):
            lower = number == 0
            inside = 0 if lower else nz - 1
            for x in range(-1, nx + 1):
                source = x * ny if 0 <= x < nx else 2 * columns + (0 if x < 0 else ny)
                zplane[k, number, pl.ds((x + 1) * pitch + 1, ny), :] = msg[pl.ds(source, ny), half]
            zplane[k, number, pl.ds(pitch, nx, stride=pitch), :] = corner[1, pl.ds(0, nx), half]
            zplane[k, number, pl.ds(pitch + ny + 1, nx, stride=pitch), :] = corner[0, pl.ds(0, nx), half]

            def layer(x, y):
                return zplane[k, number, pl.ds((x + 1) * pitch + y + 1, ny), :]

            through = {}
            for place, group in enumerate(groups):
                x, y = group
                speed, spread = end_coefficients(group, near, far)
                if x is None:
                    outer = corner[1 if y < 0 else 0, pl.ds(0, nx), half]
                    inner = edge_copy[k, pl.ds((0 if y < 0 else nx) * nz + inside, nx, stride=nz), :]
                else:
                    outer = layer(x, 0)
                    inner = copy[k, pl.ds(place * ny * nz + inside, ny, stride=nz), :]
                pair = (outer, inner) if lower else (inner, outer)
                flow = flux(speed, diff * spread, *pair)
                through[group] = flow
                rows = pl.ds(place * ny * nz + inside, ny, stride=nz)
                first[k, rows, :] = first[k, rows, :] + (flow if lower else -flow)
            behind = None
            for x in range(-1, nx):
                value = layer(x, 0)
                spread = beyond(M, x, 0, near) + beyond(M, x + 1, 0, near)
                ahead = flux(beyond(UX, x, 0, near), diff * spread, value, layer(x + 1, 0))
                if x >= 0:
                    drag = beyond(M, x, 0, near)
                    total = value + (behind - ahead)
                    total += flux(beyond(UY, x, -1, near), diff * (beyond(M, x, -1, near) + drag), layer(x, -1), value)
                    total -= flux(beyond(UY, x, 0, near), diff * (drag + beyond(M, x, 1, near)), value, layer(x, 1))
                    deep = msg[pl.ds(columns + x * ny, ny), half]
                    spread = diff * (drag + beyond(M, x, 0, far))
                    if lower:
                        total += flux(beyond(UZ, x, 0, far), spread, deep, value) - through[x, None]
                    else:
                        total += through[x, None] - flux(beyond(UZ, x, 0, near), spread, value, deep)
                    gplane[k, number, pl.ds(x * ny, ny), :] = total
                behind = ahead

        ends[k] = jnp.zeros(ends.shape[1:], F32)
        for number, (msg, corner, near, far) in enumerate(zsides):
            lower = number == 0
            inside = 0 if lower else nz - 1
            for x in range(nx):
                speed, spread = end_coefficients((x, None), near, far)
                outer = gplane[k, number, pl.ds(x * ny, ny), :]
                inner = first[k, pl.ds((x + 1) * ny * nz + inside, ny, stride=nz), :]
                pair = (outer, inner) if lower else (inner, outer)
                flow = flux(speed, diff * spread, *pair)
                ends[k, pl.ds(x * ny * nz + inside, ny, stride=nz), :] = flow if lower else -flow

        def stage(x, y):
            return first[k, pl.ds(first_row(x, y), nz), :]

        behind = [flux(at(UX, -1, y), diff * at(QX, -1, y), stage(-1, y), stage(0, y)) for y in range(ny)]
        for x in range(nx):
            below = flux(at(UY, x, -1), diff * at(QY, x, -1), stage(x, -1), stage(x, 0))
            for y in range(ny):
                value = stage(x, y)
                row = (x * ny + y) * nz
                ahead = flux(at(UX, x, y), diff * at(QX, x, y), value, stage(x + 1, y))
                above = flux(at(UY, x, y), diff * at(QY, x, y), value, stage(x, y + 1))
                total = value + (behind[y] - ahead) + (below - above)
                total += interior_z(value, at(UZ_IN, x, y), diff * at(QZ, x, y))
                total += ends[k, pl.ds(row, nz), :]
                behind[y], below = ahead, above
                out[pl.ds(row, nz), half] = 0.5 * (main(x, y) + total)


def hop(axis, step):
    peers = lax.axis_size(axis)
    return [(i, (i + step) % peers) for i in range(peers)]


def hop2(axes, steps):
    a, b = (lax.axis_size(axis) for axis in axes)
    return [
        (i * b + j, ((i + steps[0]) % a) * b + (j + steps[1]) % b) for i in range(a) for j in range(b)
    ]


def shards(species, substeps, reactants, products, rate_const, velocity, viscosity, diffusivity):
    nx, ny, nz, width = species.shape
    dims = (nx, ny, nz)
    cells, columns, face = nx * ny * nz, nx * ny, 2 * ny * nz
    reactions = reactants.shape[0]
    vmem = pl.BlockSpec(memory_space=pltpu.VMEM)
    rows = species.reshape(cells, width)
    counts = substeps.reshape(-1)
    shape = lambda *dims: pltpu.VMEM(dims, F32)
    inside = lambda value: pltpu.with_memory_space_constraint(value, pltpu.VMEM)
    params = pltpu.CompilerParams(vmem_limit_bytes=24 * 1024 * 1024)

    outside = lambda value: pltpu.with_memory_space_constraint(value, pltpu.HBM)
    anyspace = pl.BlockSpec(memory_space=pltpu.HBM)
    blocks = counts.shape[0]
    assert blocks == 4 and cells == blocks * BLOCK and face == BLOCK
    low, high, table, rows, reactants, products, rate, diff = pl.pallas_call(
        pack_x_kernel,
        out_shape=(
            shape(face + nz, width),
            shape(face + nz, width),
            shape(nx * nz, 128),
            shape(cells, width),
            pltpu.VMEM(reactants.shape, reactants.dtype),
            pltpu.VMEM(products.shape, products.dtype),
            shape(1, reactions),
            shape(1, width),
        ),
        in_specs=[anyspace] * 8,
        out_specs=(vmem,) * 8,
        scratch_shapes=[
            pltpu.VMEM((nx * 128, nz), F32),
            pltpu.VMEM(velocity.shape, F32),
            pltpu.VMEM(viscosity.shape, F32),
            pltpu.SMEM((blocks,), jnp.int32),
            pltpu.SemaphoreType.DMA((8,)),
        ],
        compiler_params=params,
        name="pack_x",
    )(
        *map(
            outside,
            (
                rows,
                counts,
                velocity,
                viscosity,
                reactants,
                products,
                rate_const.reshape(1, reactions),
                diffusivity.reshape(1, width),
            ),
        )
    )
    before = lax.ppermute(high, "gx", hop("gx", 1))
    after = lax.ppermute(low, "gx", hop("gx", -1))

    field, w_in, w_out, rate = pl.pallas_call(
        chemistry_kernel,
        out_shape=(
            shape(cells, width),
            pltpu.VMEM((reactions, 2 * width), BF16),
            pltpu.VMEM((2 * width, reactions), BF16),
            shape(reactions, 128),
        ),
        in_specs=[anyspace] + [vmem] * 4,
        out_specs=(vmem,) * 4,
        scratch_shapes=[
            pltpu.VMEM((blocks, width, BLOCK), F32),
            pltpu.SMEM((blocks,), jnp.int32),
            pltpu.SemaphoreType.DMA,
        ],
        compiler_params=params,
        name="chemistry",
    )(outside(counts), *map(inside, (rows, reactants, products, rate)))

    yrows = (2 * nx + 2) * nz + (nx + 4) // 2 * nz
    zrows = 2 * columns + 2 * ny + 16
    halo, tiles, ymsg, zlow, zhigh, yzlow, yzhigh = pl.pallas_call(
        functools.partial(pack_yz_kernel, dims),
        out_shape=(
            shape(2 * face, width),
            shape(16 * nz, 128),
            shape(2, yrows, width),
            shape(zrows, width),
            shape(zrows, width),
            shape(2, nx + 16, width),
            shape(2, nx + 16, width),
        ),
        in_specs=[vmem] * 7,
        out_specs=(vmem,) * 7,
        scratch_shapes=[
            pltpu.VMEM((width // 128 * (nx + 2) * ny * nz, 128), F32),
            pltpu.VMEM((2, width, BLOCK), F32),
        ],
        compiler_params=params,
        name="pack_yz",
    )(*map(inside, (before, after, field, table, w_in, w_out, rate)))

    zbefore = lax.ppermute(zhigh, "gz", hop("gz", 1))
    zafter = lax.ppermute(zlow, "gz", hop("gz", -1))
    if lax.axis_size("gy") == 2:
        yrecv = lax.ppermute(ymsg, "gy", hop("gy", 1))
        yzbefore = lax.ppermute(yzhigh, ("gy", "gz"), hop2(("gy", "gz"), (1, 1)))
        yzafter = lax.ppermute(yzlow, ("gy", "gz"), hop2(("gy", "gz"), (1, -1)))
    else:
        yrecv = jnp.stack([lax.ppermute(ymsg[side], "gy", hop("gy", step)) for side, step in ((0, -1), (1, 1))])
        yzbefore, yzafter = (
            jnp.stack(
                [
                    lax.ppermute(msg[side], ("gy", "gz"), hop2(("gy", "gz"), (step, zstep)))
                    for side, step in ((0, -1), (1, 1))
                ]
            )
            for msg, zstep in ((yzhigh, 1), (yzlow, -1))
        )

    halves = width // 128
    padded = (nx + 4) * 12 * nz
    grid = (nx + 2) * ny * nz
    coef, part, copy = pl.pallas_call(
        functools.partial(partial_kernel, dims),
        out_shape=(shape(8, padded, 128), shape(halves, grid, 128), shape(halves, grid, 128)),
        in_specs=[vmem] * 4,
        out_specs=(vmem,) * 3,
        compiler_params=params,
        name="partial",
    )(*map(inside, (field, halo, tiles, diff)))
    out = pl.pallas_call(
        functools.partial(transport_kernel, dims),
        out_shape=jax.ShapeDtypeStruct((cells, width), F32),
        in_specs=[vmem] * 11,
        out_specs=vmem,
        scratch_shapes=[
            pltpu.VMEM((16 * nz, 128), F32),
            pltpu.VMEM((8, padded, 128), F32),
            pltpu.VMEM((4, (nx + 2) * (ny + 2) * nz, 128), F32),
            pltpu.VMEM((halves, grid + 2 * nx * nz, 128), F32),
            pltpu.VMEM((halves, 2 * nx * nz, 128), F32),
            pltpu.VMEM((halves, 2, (nx + 2) * (ny + 2) + 8, 128), F32),
            pltpu.VMEM((halves, 2, columns, 128), F32),
            pltpu.VMEM((halves, cells, 128), F32),
        ],
        compiler_params=params,
        name="transport",
    )(*map(inside, (field, tiles, coef, part, copy, yrecv, zbefore, zafter, yzbefore, yzafter, diff)))
    return out.reshape(nx, ny, nz, width)


def solution(mesh):
    return jax.shard_map(
        shards,
        mesh=mesh,
        in_specs=(
            P("gx", "gy", "gz", None),
            P("gx", "gy", "gz"),
            P(),
            P(),
            P(),
            P(None, "gx", "gy", "gz"),
            P("gx", "gy", "gz"),
            P(),
        ),
        out_specs=P("gx", "gy", "gz", None),
        check_vma=False,
    )
```
